1024 devices in a mesh: ctx: 64 (over x, z), head: 16 (over y, core).
Axes of the slice: x: 8, y: 8, z: 8, core: 2. Of those that a mesh axis runs over, the one named last changes fastest.
Arguments:
- acts: bfloat16 [32768, 4096], P('ctx'), may hold values from -16 to 16
- queries: bfloat16 [32768, 4096], P('ctx', 'head'), may hold values from -6 to 6
- keys: bfloat16 [32768, 4096], P('ctx', 'head'), may hold values from -6 to 6
- values: bfloat16 [32768, 4096], P('ctx', 'head'), may hold values from -6 to 6
- out_grad: bfloat16 [32768, 4096], P('ctx', 'head'), may hold values from -6 to 6
Outputs:
- q_grad: bfloat16 [32768, 4096], P('ctx', 'head')
- k_grad: bfloat16 [32768, 4096], P('ctx', 'head')
- v_grad: bfloat16 [32768, 4096], P('ctx', 'head')
- wv_grad: float32 [4096, 4096], P('ctx', 'head')
The draws below stay inside these ranges and needn't reach their ends.
All inputs are finite; a program needn't handle non-finite values.
Results may differ from the reference program's by a relative error of at most 0.0064.
Values may be sent and summed in bfloat16 or wider, within the bound.
No kernel may reach another device: no remote copies, remote signals or barrier semaphores. Data moves between devices by JAX's collectives and lax.ppermute only.
A program may use at most 64 MiB of HBM per device.

```python
import jax
import jax.numpy as jnp
from jax import lax

D = 4096
HEADS = 32
DH = 128
TOK_DEV = 512
TOKENS = 32768


def spiked(entries, key, source, target, blocks, factor):
    owner, partner = [(jnp.arange(entries.shape[axis_at]) // (entries.shape[axis_at] // blocks)).reshape([-1 if axis == axis_at else 1 for axis in range(entries.ndim)]) for axis_at in (source, target)]
    chosen = jax.random.permutation(key, blocks)[partner]
    strong = (owner == chosen) | (owner == (partner + blocks // 2) % blocks)
    return jnp.where(strong, factor * entries, entries)


def level_of(stream_key, dims, cuts, least, top_value):
    factor_of, own = 1.0, jax.random.fold_in(stream_key, 6)
    for position, blocks in cuts:
        draws = jnp.exp(jax.random.uniform(jax.random.fold_in(own, position), (blocks,), jnp.float32, least / len(cuts), top_value / len(cuts)))
        factor_of = factor_of * jnp.repeat(draws, dims[position] // blocks).reshape([-1 if axis == position else 1 for axis in range(len(dims))])
    return factor_of


def bell_draw(stream_key, dims, width, most, shards=(), kind=jnp.bfloat16):
    entries = width * jax.random.normal(stream_key, dims, jnp.float32)
    if shards:
        entries = entries * level_of(stream_key, dims, shards, -0.22, 0.18)
    return jnp.clip(entries, -most, most).astype(kind)


def gaussian_with(stream_key, shape, scale, limit, shards, heavy, kind=jnp.bfloat16):
    array = scale * jax.random.normal(stream_key, shape, jnp.float32)
    if shards:
        array = array * level_of(stream_key, shape, shards, -0.22, 0.18)
    return jnp.clip(spiked(array, jax.random.fold_in(stream_key, 3), *heavy), -limit, limit).astype(kind)


def setup_inputs(seed: int = 0) -> dict:
    splits = jax.random.split(jax.random.key(seed), 6)
    return {
        "acts": gaussian_with(splits[0], (TOKENS, D), 1.0, 16.0, ((0, 64),), (0, 1, 64, 4.0)),
        "queries": bell_draw(splits[1], (TOKENS, HEADS * DH), 1.0, 6.0, ((0, 64), (1, 16))),
        "keys": bell_draw(splits[2], (TOKENS, HEADS * DH), 1.0, 6.0, ((0, 64), (1, 16))),
        "values": bell_draw(splits[3], (TOKENS, HEADS * DH), 1.0, 6.0, ((0, 64), (1, 16))),
        "out_grad": bell_draw(splits[4], (TOKENS, HEADS * DH), 1.0, 6.0, ((0, 64), (1, 16))),
    }


def normalize(block):
    full = block.astype(jnp.float32)
    factor = lax.rsqrt(lax.optimization_barrier(jnp.sum(full * full, axis=-1, keepdims=True)) + 1e-06)
    unit = full * factor
    return (unit, unit.astype(jnp.bfloat16), factor)

def project_back(unit, factor, grad_unit):
    inner = lax.optimization_barrier(jnp.sum(unit * grad_unit, axis=-1, keepdims=True))
    return (factor * (grad_unit - unit * inner)).astype(jnp.bfloat16)

def reference(acts, queries, keys, values, out_grad):
    nblocks = TOKENS // TOK_DEV
    shape_four = (nblocks, TOK_DEV, HEADS, DH)
    q_unit, q_low, q_factor = normalize(queries.reshape(shape_four))
    k_unit, k_low, k_factor = normalize(keys.reshape(shape_four))
    val_all = values.reshape(shape_four)
    grad_all = out_grad.reshape(shape_four)
    score_scale = TOKENS ** (-0.5)
    kv_local = jnp.einsum('btha,bthc->bhac', k_low.astype(jnp.float32), val_all.astype(jnp.float32))
    g_local = jnp.einsum('btha,bthc->bhac', q_low.astype(jnp.float32), grad_all.astype(jnp.float32))
    kv_state = jnp.cumsum(kv_local, axis=0) - kv_local
    g_state = lax.optimization_barrier(jnp.sum(g_local, axis=0, keepdims=True)) - jnp.cumsum(g_local, axis=0)
    causal_mask = jnp.tril(jnp.ones((TOK_DEV, TOK_DEV), dtype=bool))

    def one_block(index):
        qb = q_low[index].astype(jnp.float32)
        kb = k_low[index].astype(jnp.float32)
        vb = val_all[index].astype(jnp.float32)
        gb = grad_all[index].astype(jnp.float32)
        kv_low = kv_state[index].astype(jnp.bfloat16).astype(jnp.float32)
        g_low = g_state[index].astype(jnp.bfloat16).astype(jnp.float32)
        grad_scores = jnp.einsum('thc,shc->hts', gb, vb)
        grad_scores = jnp.where(causal_mask[None], grad_scores * score_scale, 0.0).astype(jnp.bfloat16).astype(jnp.float32)
        attn = jnp.einsum('tha,sha->hts', qb, kb)
        attn = jnp.where(causal_mask[None], attn * score_scale, 0.0).astype(jnp.bfloat16).astype(jnp.float32)
        dqn = jnp.einsum('hts,sha->tha', grad_scores, kb) + score_scale * jnp.einsum('thc,hac->tha', gb, kv_low)
        dkn = jnp.einsum('hst,sha->tha', grad_scores, qb) + score_scale * jnp.einsum('thc,hac->tha', vb, g_low)
        dvv = jnp.einsum('hst,shc->thc', attn, gb) + score_scale * jnp.einsum('tha,hac->thc', kb, g_low)
        dq_out = project_back(q_unit[index], q_factor[index], dqn)
        dk_out = project_back(k_unit[index], k_factor[index], dkn)
        return (dq_out, dk_out, dvv.astype(jnp.bfloat16))
    dq_all, dk_all, dv_all = lax.map(one_block, jnp.arange(nblocks, dtype=jnp.int32))
    flat = (TOKENS, HEADS * DH)
    dq_all = dq_all.reshape(flat)
    dk_all = dk_all.reshape(flat)
    dv_all = dv_all.reshape(flat)
    wv_grad = jnp.dot(acts.T.astype(jnp.float32), dv_all.astype(jnp.float32))
    return (dq_all, dk_all, dv_all, wv_grad)
```

```python
import functools

import jax
import jax.numpy as jnp
from jax import lax
from jax.experimental import pallas as pl
from jax.experimental.pallas import tpu as pltpu
from jax.sharding import Mesh
from jax.sharding import PartitionSpec as P

DH = 128
CTX = ("ctx_0", "ctx_1")
F32 = jnp.float32
BF16 = jnp.bfloat16


def dot(a, b, ca, cb):
    return lax.dot_general(a, b, (((ca,), (cb,)), ((), ())), preferred_element_type=F32)


def unit_of(block):
    full = block.astype(F32)
    factor = lax.rsqrt(jnp.sum(full * full, axis=-1, keepdims=True) + 1e-06)
    return full * factor, factor


def head(ref, h):
    return ref[:, h * DH : (h + 1) * DH]


def states_kernel(q_ref, k_ref, v_ref, o_ref, st_ref):
    heads = q_ref.shape[1] // DH
    rows = DH // 8
    for h in range(heads):
        kn = unit_of(head(k_ref, h))[0].astype(BF16)
        qn = unit_of(head(q_ref, h))[0].astype(BF16)
        kv = dot(kn, head(v_ref, h), 0, 0)
        g = dot(qn, head(o_ref, h), 0, 0)
        st_ref[h * rows : (h + 1) * rows] = kv.reshape(rows, 8, DH).astype(st_ref.dtype)
        at = (heads + h) * rows
        st_ref[at : at + rows] = g.reshape(rows, 8, DH).astype(st_ref.dtype)


def scan_kernel(back_ref, r_ref, out_ref):
    n = r_ref.shape[0]
    back = back_ref[0]

    def step(i, acc):
        b = jnp.where(back == 1, n - 1 - i, i)
        out_ref[b] = acc.astype(out_ref.dtype)
        return acc + r_ref[b].astype(F32)

    lax.fori_loop(0, n, step, jnp.zeros(r_ref.shape[1:], F32), unroll=8)


def local_kernel(scale, q_ref, k_ref, v_ref, o_ref, dq_ref, dk_ref, dv_ref):
    toks, width = q_ref.shape
    mask = lax.broadcasted_iota(jnp.int32, (toks, toks), 0) >= lax.broadcasted_iota(
        jnp.int32, (toks, toks), 1
    )
    for h in range(width // DH):
        at = slice(h * DH, (h + 1) * DH)
        kn = unit_of(head(k_ref, h))[0].astype(BF16)
        qn = unit_of(head(q_ref, h))[0].astype(BF16)
        v, o = head(v_ref, h), head(o_ref, h)
        attn = jnp.where(mask, dot(qn, kn, 1, 1) * scale, 0.0).astype(BF16)
        dv_ref[:, at] = dot(attn, o, 0, 0)
        scores = jnp.where(mask, dot(o, v, 1, 1) * scale, 0.0).astype(BF16)
        dq_ref[:, at] = dot(scores, kn, 1, 0)
        dk_ref[:, at] = dot(scores, qn, 0, 0)


def state(st_ref, kind, h):
    heads = st_ref.shape[0] // 2 // (DH // 8)
    rows = DH // 8
    at = (kind * heads + h) * rows
    return st_ref[at : at + rows].astype(F32).reshape(DH, DH).astype(BF16)


def weights_kernel(scale, acts_ref, k_ref, loc_ref, st_ref, dv_ref, w_ref, dvs_ref):
    @pl.when(pl.program_id(0) == 0)
    def _():
        for h in range(k_ref.shape[1] // DH):
            at = slice(h * DH, (h + 1) * DH)
            kn = unit_of(head(k_ref, h))[0].astype(BF16)
            dvv = loc_ref[:, at] + scale * dot(kn, state(st_ref, 1, h), 1, 0)
            dvs_ref[:, at] = dvv.astype(BF16)
        dv_ref[...] = dvs_ref[...]

    w_ref[...] = dot(acts_ref[...], dvs_ref[...], 0, 0).astype(w_ref.dtype)


def back_kernel(scale, q_ref, k_ref, v_ref, o_ref, lq_ref, lk_ref, st_ref, dq_ref, dk_ref):
    for h in range(q_ref.shape[1] // DH):
        at = slice(h * DH, (h + 1) * DH)
        for src, other, loc, kind, out in (
            (q_ref, o_ref, lq_ref, 0, dq_ref),
            (k_ref, v_ref, lk_ref, 1, dk_ref),
        ):
            unit, factor = unit_of(head(src, h))
            grad = loc[:, at] + scale * dot(head(other, h), state(st_ref, kind, h), 1, 1)
            inner = jnp.sum(unit * grad, axis=-1, keepdims=True)
            out[:, at] = (factor * (grad - unit * inner)).astype(BF16)


def shape(dims, dtype):
    return jax.ShapeDtypeStruct(dims, dtype)


def on_device(acts, queries, keys, values, out_grad):
    toks, width = queries.shape
    nblocks = lax.axis_size(CTX)
    scale = float(toks * nblocks) ** (-0.5)
    pieces = 2 * width // 8
    st = pl.pallas_call(
        states_kernel, out_shape=shape((pieces, 8, DH), BF16), name="states"
    )(queries, keys, values, out_grad)
    received = lax.all_to_all(st, CTX, split_axis=0, concat_axis=0, tiled=True)
    back = (lax.axis_index(CTX) >= nblocks // 2).astype(jnp.int32).reshape(1)
    answers = pl.pallas_call(
        scan_kernel,
        in_specs=[pl.BlockSpec(memory_space=pltpu.SMEM), pl.BlockSpec()],
        out_shape=shape((nblocks, 8, DH), BF16),
        name="scan",
    )(back, received)
    low = lax.all_to_all(answers, CTX, split_axis=0, concat_axis=0, tiled=True)
    part = shape((toks, width), F32)
    lq, lk, lv = pl.pallas_call(
        functools.partial(local_kernel, scale), out_shape=(part, part, part), name="local"
    )(queries, keys, values, out_grad)
    rows = acts.shape[1]
    step = 512
    whole = lambda *dims: pl.BlockSpec(dims, lambda i: (0,) * len(dims))
    dv_out, w = pl.pallas_call(
        functools.partial(weights_kernel, scale),
        grid=(rows // step,),
        in_specs=[
            pl.BlockSpec((toks, step), lambda i: (0, i)),
            whole(toks, width),
            whole(toks, width),
            whole(pieces, 8, DH),
        ],
        out_specs=(whole(toks, width), pl.BlockSpec((step, width), lambda i: (i, 0))),
        out_shape=(shape((toks, width), BF16), shape((rows, width), BF16)),
        scratch_shapes=[pltpu.VMEM((toks, width), BF16)],
        name="weights",
    )(acts, keys, lv, low)
    wv = lax.psum_scatter(w, CTX, scatter_dimension=0, tiled=True)
    dq_out, dk_out = pl.pallas_call(
        functools.partial(back_kernel, scale),
        out_shape=(shape((toks, width), BF16),) * 2,
        name="back",
    )(queries, keys, values, out_grad, lq, lk, low)
    return dq_out, dk_out, dv_out, wv.astype(F32)


def solution(mesh):
    finer = Mesh(mesh.devices.reshape(8, 8, mesh.shape["head"]), ("ctx_0", "ctx_1", "head"))
    return jax.shard_map(
        on_device,
        mesh=finer,
        in_specs=(P(CTX, None), P(CTX, "head"), P(CTX, "head"), P(CTX, "head"), P(CTX, "head")),
        out_specs=(P(CTX, "head"), P(CTX, "head"), P(CTX, "head"), P(CTX, "head")),
        check_vma=False,
    )
```

```python
import functools

import jax
import jax.numpy as jnp
from jax import lax
from jax.experimental import pallas as pl
from jax.experimental.pallas import tpu as pltpu
from jax.sharding import Mesh
from jax.sharding import PartitionSpec as P

DH = 128
CTX = ("ctx_0", "ctx_1")
MESH_AXES = CTX + ("head",)
F32 = jnp.float32
BF16 = jnp.bfloat16


def dot(a, b, ca, cb):
    return lax.dot_general(a, b, (((ca,), (cb,)), ((), ())), preferred_element_type=F32)


def unit_of(block):
    full = block.astype(F32)
    factor = lax.rsqrt(jnp.sum(full * full, axis=-1, keepdims=True) + 1e-06)
    return full * factor, factor


def head(ref, h):
    return ref[:, h * DH : (h + 1) * DH]


def states_kernel(q_ref, k_ref, v_ref, o_ref, st_ref):
    heads = q_ref.shape[1] // DH
    rows = DH // 8
    for h in range(heads):
        kn = unit_of(head(k_ref, h))[0].astype(BF16)
        qn = unit_of(head(q_ref, h))[0].astype(BF16)
        kv = dot(kn, head(v_ref, h), 0, 0)
        g = dot(qn, head(o_ref, h), 0, 0)
        st_ref[h * rows : (h + 1) * rows] = kv.reshape(rows, 8, DH).astype(st_ref.dtype)
        at = (heads + h) * rows
        st_ref[at : at + rows] = g.reshape(rows, 8, DH).astype(st_ref.dtype)


def scan_kernel(back_ref, r_ref, out_ref):
    n = r_ref.shape[0]
    back = back_ref[0]

    def step(i, acc):
        b = jnp.where(back == 1, n - 1 - i, i)
        out_ref[b] = acc.astype(out_ref.dtype)
        return acc + r_ref[b].astype(F32)

    lax.fori_loop(0, n, step, jnp.zeros(r_ref.shape[1:], F32), unroll=8)


def local_kernel(scale, q_ref, k_ref, v_ref, o_ref, dq_ref, dk_ref, dv_ref):
    toks, width = q_ref.shape
    mask = lax.broadcasted_iota(jnp.int32, (toks, toks), 0) >= lax.broadcasted_iota(
        jnp.int32, (toks, toks), 1
    )
    for h in range(width // DH):
        at = slice(h * DH, (h + 1) * DH)
        kn = unit_of(head(k_ref, h))[0].astype(BF16)
        qn = unit_of(head(q_ref, h))[0].astype(BF16)
        v, o = head(v_ref, h), head(o_ref, h)
        attn = jnp.where(mask, dot(qn, kn, 1, 1) * scale, 0.0).astype(BF16)
        dv_ref[:, at] = dot(attn, o, 0, 0)
        scores = jnp.where(mask, dot(o, v, 1, 1) * scale, 0.0).astype(BF16)
        dq_ref[:, at] = dot(scores, kn, 1, 0)
        dk_ref[:, at] = dot(scores, qn, 0, 0)


def state(st_ref, kind, h):
    heads = st_ref.shape[0] // 2 // (DH // 8)
    rows = DH // 8
    at = (kind * heads + h) * rows
    return st_ref[at : at + rows].astype(F32).reshape(DH, DH).astype(BF16)


def weights_kernel(scale, core_ref, acts_ref, k_ref, loc_ref, st_ref, dv_ref, w_ref, dvs_ref):
    i = pl.program_id(0)

    @pl.when(i == 0)
    def _():
        for h in range(k_ref.shape[1] // DH):
            at = slice(h * DH, (h + 1) * DH)
            kn = unit_of(head(k_ref, h))[0].astype(BF16)
            dvv = loc_ref[:, at] + scale * dot(kn, state(st_ref, 1, h), 1, 0)
            dvs_ref[:, at] = dvv.astype(BF16)
        dv_ref[...] = dvs_ref[...]

    part = dot(acts_ref[...], dvs_ref[...], 0, 0)
    part = part.reshape((w_ref.shape[0],) + w_ref.shape[2:]).astype(w_ref.dtype)

    @pl.when(core_ref[0] == 0)
    def _():
        w_ref[i] = part

    @pl.when(core_ref[0] == 1)
    def _():
        w_ref[:, i] = part


def back_kernel(scale, q_ref, k_ref, v_ref, o_ref, lq_ref, lk_ref, st_ref, dq_ref, dk_ref):
    for h in range(q_ref.shape[1] // DH):
        at = slice(h * DH, (h + 1) * DH)
        for src, other, loc, kind, out in (
            (q_ref, o_ref, lq_ref, 0, dq_ref),
            (k_ref, v_ref, lk_ref, 1, dk_ref),
        ):
            unit, factor = unit_of(head(src, h))
            grad = loc[:, at] + scale * dot(head(other, h), state(st_ref, kind, h), 1, 1)
            inner = jnp.sum(unit * grad, axis=-1, keepdims=True)
            out[:, at] = (factor * (grad - unit * inner)).astype(BF16)


def core_groups(nx, nz, nh):
    along_x, along_z = [], []
    for h in range(nh):
        for z in range(nz):
            along_x.append([(x * nz + z) * nh + h for x in range(nx)])
        for x in range(nx):
            along_z.append([(x * nz + z) * nh + h for z in range(nz)])
    even = lambda groups: [g for g in groups if g[0] % 2 == 0]
    odd = lambda groups: [g for g in groups if g[0] % 2 == 1]
    return even(along_x) + odd(along_z), even(along_z) + odd(along_x)


def exchange(v, groups):
    return lax.all_to_all(
        v, MESH_AXES, split_axis=0, concat_axis=0, axis_index_groups=groups, tiled=True
    )


def shape(dims, dtype):
    return jax.ShapeDtypeStruct(dims, dtype)


def on_device(acts, queries, keys, values, out_grad):
    toks, width = queries.shape
    nblocks = lax.axis_size(CTX)
    scale = float(toks * nblocks) ** (-0.5)
    pieces = 2 * width // 8
    st = pl.pallas_call(
        states_kernel, out_shape=shape((pieces, 8, DH), F32), name="states"
    )(queries, keys, values, out_grad)
    received = lax.all_to_all(st, CTX, split_axis=0, concat_axis=0, tiled=True)
    back = (lax.axis_index(CTX) >= nblocks // 2).astype(jnp.int32).reshape(1)
    answers = pl.pallas_call(
        scan_kernel,
        in_specs=[pl.BlockSpec(memory_space=pltpu.SMEM), pl.BlockSpec()],
        out_shape=shape((nblocks, 8, DH), BF16),
        name="scan",
    )(back, received)
    low = lax.all_to_all(answers, CTX, split_axis=0, concat_axis=0, tiled=True)
    part = shape((toks, width), F32)
    lq, lk, lv = pl.pallas_call(
        functools.partial(local_kernel, scale), out_shape=(part, part, part), name="local"
    )(queries, keys, values, out_grad)
    rows = acts.shape[1]
    nx, nz, nh = (lax.axis_size(a) for a in MESH_AXES)
    step = rows // nx
    own = rows // nblocks
    core = (lax.axis_index("head") % 2).astype(jnp.int32).reshape(1)
    whole = lambda *dims: pl.BlockSpec(dims, lambda i: (0,) * len(dims))
    dv_out, w = pl.pallas_call(
        functools.partial(weights_kernel, scale),
        grid=(nx,),
        in_specs=[
            pl.BlockSpec(memory_space=pltpu.SMEM),
            pl.BlockSpec((toks, step), lambda i: (0, i)),
            whole(toks, width),
            whole(toks, width),
            whole(pieces, 8, DH),
        ],
        out_specs=(whole(toks, width), whole(nx, nz, own, width)),
        out_shape=(shape((toks, width), BF16), shape((nx, nz, own, width), BF16)),
        scratch_shapes=[pltpu.VMEM((toks, width), BF16)],
        name="weights",
    )(core, acts, keys, lv, low)
    first, second = core_groups(nx, nz, nh)
    got = exchange(w, first)
    got = jnp.sum(got.astype(F32), axis=0).astype(BF16)
    got = exchange(got, second)
    wv = jnp.sum(got.astype(F32), axis=0)
    dq_out, dk_out = pl.pallas_call(
        functools.partial(back_kernel, scale),
        out_shape=(shape((toks, width), BF16),) * 2,
        name="back",
    )(queries, keys, values, out_grad, lq, lk, low)
    return dq_out, dk_out, dv_out, wv


def solution(mesh):
    finer = Mesh(mesh.devices.reshape(8, 8, mesh.shape["head"]), ("ctx_0", "ctx_1", "head"))
    return jax.shard_map(
        on_device,
        mesh=finer,
        in_specs=(P(CTX, None), P(CTX, "head"), P(CTX, "head"), P(CTX, "head"), P(CTX, "head")),
        out_specs=(P(CTX, "head"), P(CTX, "head"), P(CTX, "head"), P(CTX, "head")),
        check_vma=False,
    )
```

```python
import functools

import jax
import jax.numpy as jnp
from jax import lax
from jax.experimental import pallas as pl
from jax.experimental.pallas import tpu as pltpu
from jax.sharding import Mesh
from jax.sharding import PartitionSpec as P

DH = 128
CTX = ("ctx_0", "ctx_1")
MESH_AXES = CTX + ("head",)
ROW_CUTS = (8, 8)
F32 = jnp.float32
BF16 = jnp.bfloat16


def dot(a, b, ca, cb):
    return lax.dot_general(a, b, (((ca,), (cb,)), ((), ())), preferred_element_type=F32)


def unit_of(block):
    full = block.astype(F32)
    factor = lax.rsqrt(jnp.sum(full * full, axis=-1, keepdims=True) + 1e-06)
    return full * factor, factor


def head(ref, h):
    return ref[:, h * DH : (h + 1) * DH]


def states_kernel(q_ref, k_ref, v_ref, o_ref, st_ref):
    kn = unit_of(k_ref[...])[0].astype(BF16)
    qn = unit_of(q_ref[...])[0].astype(BF16)
    st_ref[0] = dot(kn, v_ref[...], 0, 0).reshape(st_ref.shape[1:])
    st_ref[1] = dot(qn, o_ref[...], 0, 0).reshape(st_ref.shape[1:])


def scan_kernel(back_ref, r_ref, after_ref, out_ref):
    del after_ref
    n = r_ref.shape[0]
    back = back_ref[0]

    def step(i, acc):
        b = jnp.where(back == 1, n - 1 - i, i)
        out_ref[b] = acc.astype(out_ref.dtype)
        return acc + r_ref[b].astype(F32)

    lax.fori_loop(0, n, step, jnp.zeros(r_ref.shape[1:], F32), unroll=8)


def local_kernel(scale, q_ref, k_ref, v_ref, o_ref, dq_ref, dk_ref, dv_ref, kn_ref):
    toks, width = q_ref.shape
    mask = lax.broadcasted_iota(jnp.int32, (toks, toks), 0) >= lax.broadcasted_iota(
        jnp.int32, (toks, toks), 1
    )
    for h in range(width // DH):
        at = slice(h * DH, (h + 1) * DH)
        kn = unit_of(head(k_ref, h))[0].astype(BF16)
        kn_ref[:, at] = kn
        qn = unit_of(head(q_ref, h))[0].astype(BF16)
        v, o = head(v_ref, h), head(o_ref, h)
        attn = jnp.where(mask, dot(qn, kn, 1, 1) * scale, 0.0).astype(BF16)
        dv_ref[:, at] = dot(attn, o, 0, 0)
        scores = jnp.where(mask, dot(o, v, 1, 1) * scale, 0.0).astype(BF16)
        dq_ref[:, at] = dot(scores, kn, 1, 0)
        dk_ref[:, at] = dot(scores, qn, 0, 0)


def state(st_ref, kind, h):
    heads = st_ref.shape[0] // 2 // (DH // 8)
    rows = DH // 8
    at = (kind * heads + h) * rows
    return st_ref[at : at + rows].astype(F32).reshape(DH, DH).astype(BF16)


def turn_kernel(core_ref, acts_ref, out_ref):
    x = pl.program_id(0)
    nx = pl.num_programs(0)
    nz, own = ROW_CUTS[1], out_ref.shape[2]
    turned = acts_ref[...].T.reshape(nz, own, acts_ref.shape[0])
    for core in range(2):

        @pl.when(core_ref[0] == core)
        def _():
            for z in range(nz):
                near, far = place(lax.rem(x + nx - core, nx), (z + nz - core) % nz, nz)
                out_ref[near, far] = turned[z]


def weights_kernel(scale, turned_ref, kn_ref, loc_ref, st_ref, dv_ref, w_ref, dvs_ref):
    @pl.when(pl.program_id(0) == 0)
    def _():
        for h in range(kn_ref.shape[1] // DH):
            at = slice(h * DH, (h + 1) * DH)
            dvv = loc_ref[:, at] + scale * dot(head(kn_ref, h), state(st_ref, 1, h), 1, 0)
            dvs_ref[:, at] = dvv.astype(BF16)
        dv_ref[...] = dvs_ref[...]

    w_ref[...] = dot(turned_ref[...], dvs_ref[...], 1, 0).astype(w_ref.dtype)


def back_kernel(scale, q_ref, k_ref, v_ref, o_ref, lq_ref, lk_ref, st_ref, dq_ref, dk_ref):
    for h in range(q_ref.shape[1] // DH):
        at = slice(h * DH, (h + 1) * DH)
        for src, other, loc, kind, out in (
            (q_ref, o_ref, lq_ref, 0, dq_ref),
            (k_ref, v_ref, lk_ref, 1, dk_ref),
        ):
            unit, factor = unit_of(head(src, h))
            grad = loc[:, at] + scale * dot(head(other, h), state(st_ref, kind, h), 1, 1)
            inner = jnp.sum(unit * grad, axis=-1, keepdims=True)
            out[:, at] = (factor * (grad - unit * inner)).astype(BF16)


def place(x, z, nz):
    return x % 2 * 2 + z % 2, x // 2 * (nz // 2) + z // 2


def core_groups(nx, nz, nh):
    squares, likes = {}, {}
    for h in range(nh):
        core = h % 2
        for x in range(nx):
            for z in range(nz):
                near, far = place((x + nx - core) % nx, (z + nz - core) % nz, nz)
                device = (x * nz + z) * nh + h
                squares.setdefault((h, far), {})[near] = device
                likes.setdefault((h, near), {})[far] = device
    ordered = lambda groups: [[g[i] for i in range(len(g))] for g in groups.values()]
    return ordered(squares), ordered(likes)


def exchange(v, groups):
    return lax.all_to_all(
        v, MESH_AXES, split_axis=0, concat_axis=0, axis_index_groups=groups, tiled=True
    )


def shape(dims, dtype):
    return jax.ShapeDtypeStruct(dims, dtype)


def on_device(acts, queries, keys, values, out_grad):
    toks, width = queries.shape
    nblocks = lax.axis_size(CTX)
    scale = float(toks * nblocks) ** (-0.5)
    pieces = 2 * width // 8
    heads = width // DH
    of_head = pl.BlockSpec((toks, DH), lambda h: (0, h))
    st = pl.pallas_call(
        states_kernel,
        grid=(heads,),
        in_specs=[of_head] * 4,
        out_specs=pl.BlockSpec((2, DH // 8, 8, DH), lambda h: (0, h, 0, 0)),
        out_shape=shape((2, heads * DH // 8, 8, DH), F32),
        name="states",
    )(queries, keys, values, out_grad).reshape(pieces, 8, DH)
    rows = acts.shape[1]
    nx, nz, nh = (lax.axis_size(a) for a in MESH_AXES)
    step = rows // nx
    own = rows // nblocks
    core = (lax.axis_index("head") % 2).astype(jnp.int32).reshape(1)
    whole = lambda *dims: pl.BlockSpec(dims, lambda i: (0,) * len(dims))
    cut = (4, nblocks // 4, own)
    turned = pl.pallas_call(
        turn_kernel,
        grid=(nx,),
        in_specs=[
            pl.BlockSpec(memory_space=pltpu.SMEM),
            pl.BlockSpec((toks, step), lambda i: (0, i)),
        ],
        out_specs=whole(*cut, toks),
        out_shape=shape((*cut, toks), BF16),
        name="turn",
    )(core, acts)
    received = lax.all_to_all(st, CTX, split_axis=0, concat_axis=0, tiled=True)
    back = (lax.axis_index(CTX) >= nblocks // 2).astype(jnp.int32).reshape(1)
    answers = pl.pallas_call(
        scan_kernel,
        in_specs=[
            pl.BlockSpec(memory_space=pltpu.SMEM),
            pl.BlockSpec(memory_space=pltpu.VMEM),
            pl.BlockSpec(memory_space=pl.ANY),
        ],
        out_shape=shape((nblocks, 8, DH), BF16),
        name="scan",
    )(back, pltpu.with_memory_space_constraint(received, pltpu.VMEM), turned)
    low = lax.all_to_all(answers, CTX, split_axis=0, concat_axis=0, tiled=True)
    low = pltpu.with_memory_space_constraint(low, pltpu.VMEM)
    part = shape((toks, width), F32)
    lq, lk, lv, kn = pl.pallas_call(
        functools.partial(local_kernel, scale),
        out_shape=(part, part, part, shape((toks, width), BF16)),
        name="local",
    )(queries, keys, values, out_grad)
    dv_out, w = pl.pallas_call(
        functools.partial(weights_kernel, scale),
        grid=(rows // step,),
        in_specs=[
            pl.BlockSpec((step, toks), lambda i: (i, 0)),
            whole(toks, width),
            whole(toks, width),
            pl.BlockSpec(memory_space=pltpu.VMEM),
        ],
        out_specs=(whole(toks, width), pl.BlockSpec((step, width), lambda i: (i, 0))),
        out_shape=(shape((toks, width), BF16), shape((rows, width), BF16)),
        scratch_shapes=[pltpu.VMEM((toks, width), BF16)],
        name="weights",
    )(turned.reshape(rows, toks), kn, lv, low)
    w = w.reshape(*cut, width)
    first, second = core_groups(nx, nz, nh)
    got = exchange(w, first)
    got = jnp.sum(got.astype(F32), axis=0).astype(BF16)
    got = exchange(got, second)
    wv = jnp.sum(got.astype(F32), axis=0)
    dq_out, dk_out = pl.pallas_call(
        functools.partial(back_kernel, scale),
        in_specs=[pl.BlockSpec(memory_space=pltpu.VMEM)] * 7,
        out_shape=(shape((toks, width), BF16),) * 2,
        name="back",
    )(queries, keys, values, out_grad, lq, lk, low)
    return dq_out, dk_out, dv_out, wv


def solution(mesh):
    finer = Mesh(mesh.devices.reshape(*ROW_CUTS, mesh.shape["head"]), ("ctx_0", "ctx_1", "head"))
    return jax.shard_map(
        on_device,
        mesh=finer,
        in_specs=(P(CTX, None), P(CTX, "head"), P(CTX, "head"), P(CTX, "head"), P(CTX, "head")),
        out_specs=(P(CTX, "head"), P(CTX, "head"), P(CTX, "head"), P(CTX, "head")),
        check_vma=False,
    )
```

```python
import functools

import jax
import jax.numpy as jnp
from jax import lax
from jax.experimental import pallas as pl
from jax.experimental.pallas import tpu as pltpu
from jax.sharding import Mesh
from jax.sharding import PartitionSpec as P

DH = 128
CTX = ("ctx_0", "ctx_1")
MESH_AXES = CTX + ("head",)
ROW_CUTS = (8, 8)
IN_VMEM = pl.BlockSpec(memory_space=pltpu.VMEM)
F32 = jnp.float32
BF16 = jnp.bfloat16


def dot(a, b, ca, cb):
    return lax.dot_general(a, b, (((ca,), (cb,)), ((), ())), preferred_element_type=F32)


def unit_of(block):
    full = block.astype(F32)
    factor = lax.rsqrt(jnp.sum(full * full, axis=-1, keepdims=True) + 1e-06)
    return full * factor, factor


def head(ref, h):
    return ref[:, h * DH : (h + 1) * DH]


def states_kernel(q_ref, k_ref, v_ref, o_ref, st_ref):
    kn = unit_of(k_ref[...])[0].astype(BF16)
    qn = unit_of(q_ref[...])[0].astype(BF16)
    st_ref[0] = dot(kn, v_ref[...], 0, 0).reshape(st_ref.shape[1:])
    st_ref[1] = dot(qn, o_ref[...], 0, 0).reshape(st_ref.shape[1:])


def scan_kernel(back_ref, r_ref, after_ref, out_ref):
    del after_ref
    n = r_ref.shape[0]
    back = back_ref[0]

    def step(i, acc):
        b = jnp.where(back == 1, n - 1 - i, i)
        out_ref[b] = acc.astype(out_ref.dtype)
        return acc + r_ref[b].astype(F32)

    lax.fori_loop(0, n, step, jnp.zeros(r_ref.shape[1:], F32), unroll=8)


def local_kernel(scale, q_ref, k_ref, v_ref, o_ref, dq_ref, dk_ref, dv_ref, kn_ref):
    toks, width = q_ref.shape
    mask = lax.broadcasted_iota(jnp.int32, (toks, toks), 0) >= lax.broadcasted_iota(
        jnp.int32, (toks, toks), 1
    )
    for h in range(width // DH):
        at = slice(h * DH, (h + 1) * DH)
        kn = unit_of(head(k_ref, h))[0].astype(BF16)
        kn_ref[:, at] = kn
        qn = unit_of(head(q_ref, h))[0].astype(BF16)
        v, o = head(v_ref, h), head(o_ref, h)
        attn = jnp.where(mask, dot(qn, kn, 1, 1) * scale, 0.0).astype(BF16)
        dv_ref[:, at] = dot(attn, o, 0, 0)
        scores = jnp.where(mask, dot(o, v, 1, 1) * scale, 0.0).astype(BF16)
        dq_ref[:, at] = dot(scores, kn, 1, 0)
        dk_ref[:, at] = dot(scores, qn, 0, 0)


def state(st_ref, kind, h):
    heads = st_ref.shape[0] // 2 // (DH // 8)
    rows = DH // 8
    at = (kind * heads + h) * rows
    return st_ref[at : at + rows].astype(F32).reshape(DH, DH).astype(BF16)


def turn_kernel(core_ref, acts_ref, out_ref):
    x = pl.program_id(0)
    nx = pl.num_programs(0)
    nz, own = ROW_CUTS[1], out_ref.shape[2]
    turned = acts_ref[...].T.reshape(nz, own, acts_ref.shape[0])
    for core in range(2):

        @pl.when(core_ref[0] == core)
        def _():
            for z in range(nz):
                near, far = place(lax.rem(x + nx - core, nx), (z + nz - core) % nz, nz)
                out_ref[near, far] = turned[z]


def weights_kernel(
    scale, turned_ref, kn_ref, loc_ref, st_ref, dv_ref, w_ref, rows_ref, low_ref, sums_ref, come, go
):
    n = come.shape[0]
    step = rows_ref.shape[0] // n
    at_step = lambda i: pl.ds(i * step, step)
    coming = [
        pltpu.make_async_copy(turned_ref.at[at_step(i)], rows_ref.at[at_step(i)], come.at[i])
        for i in range(n)
    ]
    going = [
        pltpu.make_async_copy(sums_ref.at[at_step(i)], w_ref.at[at_step(i)], go.at[i])
        for i in range(n)
    ]
    for copy in coming:
        copy.start()
    for h in range(kn_ref.shape[1] // DH):
        at = slice(h * DH, (h + 1) * DH)
        dvv = loc_ref[:, at] + scale * dot(head(kn_ref, h), state(st_ref, 1, h), 1, 0)
        low_ref[:, at] = dvv.astype(BF16)
    kept = pltpu.make_async_copy(low_ref, dv_ref, go.at[n])
    kept.start()
    for i in range(n):
        coming[i].wait()
        sums_ref[at_step(i)] = dot(rows_ref[at_step(i)], low_ref[...], 1, 0).astype(BF16)
        going[i].start()
    for copy in going:
        copy.wait()
    kept.wait()


def back_kernel(scale, q_ref, k_ref, v_ref, o_ref, lq_ref, lk_ref, st_ref, dq_ref, dk_ref):
    for h in range(q_ref.shape[1] // DH):
        at = slice(h * DH, (h + 1) * DH)
        for src, other, loc, kind, out in (
            (q_ref, o_ref, lq_ref, 0, dq_ref),
            (k_ref, v_ref, lk_ref, 1, dk_ref),
        ):
            unit, factor = unit_of(head(src, h))
            grad = loc[:, at] + scale * dot(head(other, h), state(st_ref, kind, h), 1, 1)
            inner = jnp.sum(unit * grad, axis=-1, keepdims=True)
            out[:, at] = (factor * (grad - unit * inner)).astype(BF16)


def place(x, z, nz):
    return x % 2 * 2 + z % 2, x // 2 * (nz // 2) + z // 2


def core_groups(nx, nz, nh):
    squares, likes = {}, {}
    for h in range(nh):
        core = h % 2
        for x in range(nx):
            for z in range(nz):
                near, far = place((x + nx - core) % nx, (z + nz - core) % nz, nz)
                device = (x * nz + z) * nh + h
                squares.setdefault((h, far), {})[near] = device
                likes.setdefault((h, near), {})[far] = device
    ordered = lambda groups: [[g[i] for i in range(len(g))] for g in groups.values()]
    return ordered(squares), ordered(likes)


def exchange(v, groups):
    return lax.all_to_all(
        v, MESH_AXES, split_axis=0, concat_axis=0, axis_index_groups=groups, tiled=True
    )


def in_vmem(v):
    return pltpu.with_memory_space_constraint(v, pltpu.VMEM)


def shape(dims, dtype):
    return jax.ShapeDtypeStruct(dims, dtype)


def on_device(acts, queries, keys, values, out_grad):
    toks, width = queries.shape
    nblocks = lax.axis_size(CTX)
    scale = float(toks * nblocks) ** (-0.5)
    pieces = 2 * width // 8
    heads = width // DH
    of_head = pl.BlockSpec((toks, DH), lambda h: (0, h))
    st = pl.pallas_call(
        states_kernel,
        grid=(heads,),
        in_specs=[of_head] * 4,
        out_specs=pl.BlockSpec((2, DH // 8, 8, DH), lambda h: (0, h, 0, 0)),
        out_shape=shape((2, heads * DH // 8, 8, DH), F32),
        name="states",
    )(queries, keys, values, out_grad).reshape(pieces, 8, DH)
    rows = acts.shape[1]
    nx, nz, nh = (lax.axis_size(a) for a in MESH_AXES)
    step = rows // nx
    own = rows // nblocks
    core = (lax.axis_index("head") % 2).astype(jnp.int32).reshape(1)
    whole = lambda *dims: pl.BlockSpec(dims, lambda i: (0,) * len(dims))
    cut = (4, nblocks // 4, own)
    turned = pl.pallas_call(
        turn_kernel,
        grid=(nx,),
        in_specs=[
            pl.BlockSpec(memory_space=pltpu.SMEM),
            pl.BlockSpec((toks, step), lambda i: (0, i)),
        ],
        out_specs=whole(*cut, toks),
        out_shape=shape((*cut, toks), BF16),
        name="turn",
    )(core, acts)
    received = lax.all_to_all(st, CTX, split_axis=0, concat_axis=0, tiled=True)
    back = (lax.axis_index(CTX) >= nblocks // 2).astype(jnp.int32).reshape(1)
    answers = pl.pallas_call(
        scan_kernel,
        in_specs=[
            pl.BlockSpec(memory_space=pltpu.SMEM),
            IN_VMEM,
            pl.BlockSpec(memory_space=pl.ANY),
        ],
        out_shape=shape((nblocks, 8, DH), BF16),
        name="scan",
    )(back, in_vmem(received), turned)
    low = lax.all_to_all(answers, CTX, split_axis=0, concat_axis=0, tiled=True)
    low = in_vmem(low)
    part = shape((toks, width), F32)
    lq, lk, lv, kn = pl.pallas_call(
        functools.partial(local_kernel, scale),
        out_shape=(part, part, pltpu.VMEM((toks, width), F32), pltpu.VMEM((toks, width), BF16)),
        name="local",
    )(queries, keys, values, out_grad)
    anywhere = pl.BlockSpec(memory_space=pl.ANY)
    dv_out, w = pl.pallas_call(
        functools.partial(weights_kernel, scale),
        in_specs=[anywhere, IN_VMEM, IN_VMEM, IN_VMEM],
        out_specs=(anywhere, anywhere),
        out_shape=(shape((toks, width), BF16), shape((rows, width), BF16)),
        scratch_shapes=[
            pltpu.VMEM((rows, toks), BF16),
            pltpu.VMEM((toks, width), BF16),
            pltpu.VMEM((rows, width), BF16),
            pltpu.SemaphoreType.DMA((nx,)),
            pltpu.SemaphoreType.DMA((nx + 1,)),
        ],
        name="weights",
    )(turned.reshape(rows, toks), in_vmem(kn), in_vmem(lv), low)
    w = w.reshape(*cut, width)
    first, second = core_groups(nx, nz, nh)
    got = exchange(w, first)
    got = jnp.sum(got.astype(F32), axis=0).astype(BF16)
    got = exchange(got, second)
    wv = jnp.sum(got.astype(F32), axis=0)
    dq_out, dk_out = pl.pallas_call(
        functools.partial(back_kernel, scale),
        in_specs=[IN_VMEM] * 7,
        out_shape=(shape((toks, width), BF16),) * 2,
        name="back",
    )(queries, keys, values, out_grad, lq, lk, low)
    return dq_out, dk_out, dv_out, wv


def solution(mesh):
    finer = Mesh(mesh.devices.reshape(*ROW_CUTS, mesh.shape["head"]), ("ctx_0", "ctx_1", "head"))
    return jax.shard_map(
        on_device,
        mesh=finer,
        in_specs=(P(CTX, None), P(CTX, "head"), P(CTX, "head"), P(CTX, "head"), P(CTX, "head")),
        out_specs=(P(CTX, "head"), P(CTX, "head"), P(CTX, "head"), P(CTX, "head")),
        check_vma=False,
    )
```

```python
import functools

import jax
import jax.numpy as jnp
from jax import lax
from jax.experimental import pallas as pl
from jax.experimental.pallas import tpu as pltpu
from jax.sharding import Mesh
from jax.sharding import PartitionSpec as P

DH = 128
CTX = ("ctx_0", "ctx_1")
ROW_CUTS = (8, 8)
IN_VMEM = pl.BlockSpec(memory_space=pltpu.VMEM)
F32 = jnp.float32
BF16 = jnp.bfloat16


def dot(a, b, ca, cb):
    return lax.dot_general(a, b, (((ca,), (cb,)), ((), ())), preferred_element_type=F32)


def unit_of(block):
    full = block.astype(F32)
    factor = lax.rsqrt(jnp.sum(full * full, axis=-1, keepdims=True) + 1e-06)
    return full * factor, factor


def head(ref, h):
    return ref[:, h * DH : (h + 1) * DH]


def states_kernel(q_ref, k_ref, v_ref, o_ref, st_ref):
    kn = unit_of(k_ref[...])[0].astype(BF16)
    qn = unit_of(q_ref[...])[0].astype(BF16)
    st_ref[0] = dot(kn, v_ref[...], 0, 0).reshape(st_ref.shape[1:])
    st_ref[1] = dot(qn, o_ref[...], 0, 0).reshape(st_ref.shape[1:])


def scan_kernel(back_ref, r_ref, after_ref, out_ref):
    del after_ref
    n = r_ref.shape[0]
    back = back_ref[0]

    def step(i, acc):
        b = jnp.where(back == 1, n - 1 - i, i)
        out_ref[b] = acc.astype(out_ref.dtype)
        return acc + r_ref[b].astype(F32)

    lax.fori_loop(0, n, step, jnp.zeros(r_ref.shape[1:], F32), unroll=8)


def local_kernel(scale, q_ref, k_ref, v_ref, o_ref, dq_ref, dk_ref, dv_ref, kn_ref):
    toks, width = q_ref.shape
    mask = lax.broadcasted_iota(jnp.int32, (toks, toks), 0) >= lax.broadcasted_iota(
        jnp.int32, (toks, toks), 1
    )
    for h in range(width // DH):
        at = slice(h * DH, (h + 1) * DH)
        kn = unit_of(head(k_ref, h))[0].astype(BF16)
        kn_ref[:, at] = kn
        qn = unit_of(head(q_ref, h))[0].astype(BF16)
        v, o = head(v_ref, h), head(o_ref, h)
        attn = jnp.where(mask, dot(qn, kn, 1, 1) * scale, 0.0).astype(BF16)
        dv_ref[:, at] = dot(attn, o, 0, 0)
        scores = jnp.where(mask, dot(o, v, 1, 1) * scale, 0.0).astype(BF16)
        dq_ref[:, at] = dot(scores, kn, 1, 0)
        dk_ref[:, at] = dot(scores, qn, 0, 0)


def state(st_ref, kind, h):
    heads = st_ref.shape[0] // 2 // (DH // 8)
    rows = DH // 8
    at = (kind * heads + h) * rows
    return st_ref[at : at + rows].astype(F32).reshape(DH, DH).astype(BF16)


def turn_kernel(acts_ref, out_ref):
    out_ref[...] = acts_ref[...].T


def weights_kernel(
    scale, turned_ref, kn_ref, loc_ref, st_ref, dv_ref, w_ref, rows_ref, low_ref, sums_ref, come, go
):
    n = come.shape[0]
    step = rows_ref.shape[0] // n
    at_step = lambda i: pl.ds(i * step, step)
    coming = [
        pltpu.make_async_copy(turned_ref.at[at_step(i)], rows_ref.at[at_step(i)], come.at[i])
        for i in range(n)
    ]
    going = [
        pltpu.make_async_copy(sums_ref.at[at_step(i)], w_ref.at[at_step(i)], go.at[i])
        for i in range(n)
    ]
    for copy in coming:
        copy.start()
    for h in range(kn_ref.shape[1] // DH):
        at = slice(h * DH, (h + 1) * DH)
        dvv = loc_ref[:, at] + scale * dot(head(kn_ref, h), state(st_ref, 1, h), 1, 0)
        low_ref[:, at] = dvv.astype(BF16)
    kept = pltpu.make_async_copy(low_ref, dv_ref, go.at[n])
    kept.start()
    for i in range(n):
        coming[i].wait()
        sums_ref[at_step(i)] = dot(rows_ref[at_step(i)], low_ref[...], 1, 0).astype(BF16)
        going[i].start()
    for copy in going:
        copy.wait()
    kept.wait()


def back_kernel(scale, q_ref, k_ref, v_ref, o_ref, lq_ref, lk_ref, st_ref, dq_ref, dk_ref):
    for h in range(q_ref.shape[1] // DH):
        at = slice(h * DH, (h + 1) * DH)
        for src, other, loc, kind, out in (
            (q_ref, o_ref, lq_ref, 0, dq_ref),
            (k_ref, v_ref, lk_ref, 1, dk_ref),
        ):
            unit, factor = unit_of(head(src, h))
            grad = loc[:, at] + scale * dot(head(other, h), state(st_ref, kind, h), 1, 1)
            inner = jnp.sum(unit * grad, axis=-1, keepdims=True)
            out[:, at] = (factor * (grad - unit * inner)).astype(BF16)


def in_vmem(v):
    return pltpu.with_memory_space_constraint(v, pltpu.VMEM)


def shape(dims, dtype):
    return jax.ShapeDtypeStruct(dims, dtype)


def on_device(acts, queries, keys, values, out_grad):
    toks, width = queries.shape
    nblocks = lax.axis_size(CTX)
    scale = float(toks * nblocks) ** (-0.5)
    pieces = 2 * width // 8
    heads = width // DH
    of_head = pl.BlockSpec((toks, DH), lambda h: (0, h))
    st = pl.pallas_call(
        states_kernel,
        grid=(heads,),
        in_specs=[of_head] * 4,
        out_specs=pl.BlockSpec((2, DH // 8, 8, DH), lambda h: (0, h, 0, 0)),
        out_shape=shape((2, heads * DH // 8, 8, DH), F32),
        name="states",
    )(queries, keys, values, out_grad).reshape(pieces, 8, DH)
    rows = acts.shape[1]
    own = rows // nblocks
    steps = 8
    turned = pl.pallas_call(
        turn_kernel,
        grid=(steps,),
        in_specs=[pl.BlockSpec((toks, rows // steps), lambda i: (0, i))],
        out_specs=pl.BlockSpec((rows // steps, toks), lambda i: (i, 0)),
        out_shape=shape((rows, toks), BF16),
        name="turn",
    )(acts)
    received = lax.all_to_all(st, CTX, split_axis=0, concat_axis=0, tiled=True)
    back = (lax.axis_index(CTX) >= nblocks // 2).astype(jnp.int32).reshape(1)
    answers = pl.pallas_call(
        scan_kernel,
        in_specs=[
            pl.BlockSpec(memory_space=pltpu.SMEM),
            IN_VMEM,
            pl.BlockSpec(memory_space=pl.ANY),
        ],
        out_shape=shape((nblocks, 8, DH), BF16),
        name="scan",
    )(back, in_vmem(received), turned)
    low = lax.all_to_all(answers, CTX, split_axis=0, concat_axis=0, tiled=True)
    low = in_vmem(low)
    part = shape((toks, width), F32)
    lq, lk, lv, kn = pl.pallas_call(
        functools.partial(local_kernel, scale),
        out_shape=(part, part, pltpu.VMEM((toks, width), F32), pltpu.VMEM((toks, width), BF16)),
        name="local",
    )(queries, keys, values, out_grad)
    anywhere = pl.BlockSpec(memory_space=pl.ANY)
    dv_out, w = pl.pallas_call(
        functools.partial(weights_kernel, scale),
        in_specs=[anywhere, IN_VMEM, IN_VMEM, IN_VMEM],
        out_specs=(anywhere, anywhere),
        out_shape=(shape((toks, width), BF16), shape((rows, width), BF16)),
        scratch_shapes=[
            pltpu.VMEM((rows, toks), BF16),
            pltpu.VMEM((toks, width), BF16),
            pltpu.VMEM((rows, width), BF16),
            pltpu.SemaphoreType.DMA((steps,)),
            pltpu.SemaphoreType.DMA((steps + 1,)),
        ],
        name="weights",
    )(turned, in_vmem(kn), in_vmem(lv), low)
    got = lax.all_to_all(
        w.reshape(nblocks, own, width), CTX, split_axis=0, concat_axis=0, tiled=True
    )
    wv = jnp.sum(got.astype(F32), axis=0)
    dq_out, dk_out = pl.pallas_call(
        functools.partial(back_kernel, scale),
        in_specs=[IN_VMEM] * 7,
        out_shape=(shape((toks, width), BF16),) * 2,
        name="back",
    )(queries, keys, values, out_grad, lq, lk, low)
    return dq_out, dk_out, dv_out, wv


def solution(mesh):
    finer = Mesh(mesh.devices.reshape(*ROW_CUTS, mesh.shape["head"]), ("ctx_0", "ctx_1", "head"))
    return jax.shard_map(
        on_device,
        mesh=finer,
        in_specs=(P(CTX, None), P(CTX, "head"), P(CTX, "head"), P(CTX, "head"), P(CTX, "head")),
        out_specs=(P(CTX, "head"), P(CTX, "head"), P(CTX, "head"), P(CTX, "head")),
        check_vma=False,
    )
```

```python
import functools

import jax
import jax.numpy as jnp
from jax import lax
from jax.experimental import pallas as pl
from jax.experimental.pallas import tpu as pltpu
from jax.sharding import Mesh
from jax.sharding import PartitionSpec as P

DH = 128
CTX = ("ctx_0", "ctx_1")
MESH_AXES = CTX + ("head",)
ROW_CUTS = (8, 8)
IN_VMEM = pl.BlockSpec(memory_space=pltpu.VMEM)
F32 = jnp.float32
BF16 = jnp.bfloat16


def dot(a, b, ca, cb):
    return lax.dot_general(a, b, (((ca,), (cb,)), ((), ())), preferred_element_type=F32)


def unit_of(block):
    full = block.astype(F32)
    factor = lax.rsqrt(jnp.sum(full * full, axis=-1, keepdims=True) + 1e-06)
    return full * factor, factor


def head(ref, h):
    return ref[:, h * DH : (h + 1) * DH]


def states_kernel(q_ref, k_ref, v_ref, o_ref, st_ref):
    kn = unit_of(k_ref[...])[0].astype(BF16)
    qn = unit_of(q_ref[...])[0].astype(BF16)
    st_ref[0] = dot(kn, v_ref[...], 0, 0).reshape(st_ref.shape[1:])
    st_ref[1] = dot(qn, o_ref[...], 0, 0).reshape(st_ref.shape[1:])


def scan_kernel(back_ref, r_ref, after_ref, out_ref):
    del after_ref
    n = r_ref.shape[0]
    back = back_ref[0]

    def step(i, acc):
        b = jnp.where(back == 1, n - 1 - i, i)
        out_ref[b] = acc.astype(out_ref.dtype)
        return acc + r_ref[b].astype(F32)

    lax.fori_loop(0, n, step, jnp.zeros(r_ref.shape[1:], F32), unroll=8)


def local_kernel(scale, q_ref, k_ref, v_ref, o_ref, dq_ref, dk_ref, dv_ref, kn_ref):
    toks, width = q_ref.shape
    mask = lax.broadcasted_iota(jnp.int32, (toks, toks), 0) >= lax.broadcasted_iota(
        jnp.int32, (toks, toks), 1
    )
    for h in range(width // DH):
        at = slice(h * DH, (h + 1) * DH)
        kn = unit_of(head(k_ref, h))[0].astype(BF16)
        kn_ref[:, at] = kn
        qn = unit_of(head(q_ref, h))[0].astype(BF16)
        v, o = head(v_ref, h), head(o_ref, h)
        attn = jnp.where(mask, dot(qn, kn, 1, 1) * scale, 0.0).astype(BF16)
        dv_ref[:, at] = dot(attn, o, 0, 0)
        scores = jnp.where(mask, dot(o, v, 1, 1) * scale, 0.0).astype(BF16)
        dq_ref[:, at] = dot(scores, kn, 1, 0)
        dk_ref[:, at] = dot(scores, qn, 0, 0)


def state(st_ref, kind, h):
    heads = st_ref.shape[0] // 2 // (DH // 8)
    rows = DH // 8
    at = (kind * heads + h) * rows
    return st_ref[at : at + rows].astype(F32).reshape(DH, DH).astype(BF16)


def turn_kernel(core_ref, acts_ref, kept_ref, out_ref):
    x = pl.program_id(0)
    nx = pl.num_programs(0)
    nz, own = ROW_CUTS[1], out_ref.shape[2]
    half = out_ref.shape[0]
    turned = acts_ref[...].T.reshape(nz, own, acts_ref.shape[0])
    for core in range(2):
        for z in range(nz):
            near, far = place(lax.rem(x + nx - core, nx), (z + nz - core) % nz, nz)

            @pl.when((core_ref[0] == core) & (near < half))
            def _():
                kept_ref[near, far] = turned[z]

            @pl.when((core_ref[0] == core) & (near >= half))
            def _():
                out_ref[near - half, far] = turned[z]


def weights_kernel(
    scale, kept_ref, turned_ref, kn_ref, loc_ref, st_ref, dv_ref, w_ref, rows_ref, low_ref, sums_ref, come, go
):
    n = come.shape[0]
    step = rows_ref.shape[0] // n
    at_step = lambda i: pl.ds(i * step, step)
    coming = [
        pltpu.make_async_copy(turned_ref.at[at_step(i)], rows_ref.at[at_step(i)], come.at[i])
        for i in range(n)
    ]
    going = [
        pltpu.make_async_copy(sums_ref.at[at_step(i)], w_ref.at[at_step(i)], go.at[i])
        for i in range(2 * n)
    ]
    for copy in coming:
        copy.start()
    for h in range(kn_ref.shape[1] // DH):
        at = slice(h * DH, (h + 1) * DH)
        dvv = loc_ref[:, at] + scale * dot(head(kn_ref, h), state(st_ref, 1, h), 1, 0)
        low_ref[:, at] = dvv.astype(BF16)
    keep = pltpu.make_async_copy(low_ref, dv_ref, go.at[2 * n])
    keep.start()
    for i in range(2 * n):
        if i < n:
            rows = kept_ref[at_step(i)]
        else:
            coming[i - n].wait()
            rows = rows_ref[at_step(i - n)]
        sums_ref[at_step(i)] = dot(rows, low_ref[...], 1, 0).astype(BF16)
        going[i].start()
    for copy in going:
        copy.wait()
    keep.wait()


def back_kernel(scale, q_ref, k_ref, v_ref, o_ref, lq_ref, lk_ref, st_ref, dq_ref, dk_ref):
    for h in range(q_ref.shape[1] // DH):
        at = slice(h * DH, (h + 1) * DH)
        for src, other, loc, kind, out in (
            (q_ref, o_ref, lq_ref, 0, dq_ref),
            (k_ref, v_ref, lk_ref, 1, dk_ref),
        ):
            unit, factor = unit_of(head(src, h))
            grad = loc[:, at] + scale * dot(head(other, h), state(st_ref, kind, h), 1, 1)
            inner = jnp.sum(unit * grad, axis=-1, keepdims=True)
            out[:, at] = (factor * (grad - unit * inner)).astype(BF16)


def place(x, z, nz):
    flip = nz // 2
    return (
        (x + x // flip) % 2 * 2 + (z + z // flip) % 2,
        x // 2 * (nz // 2) + z // 2,
    )


def core_groups(nx, nz, nh):
    squares, likes = {}, {}
    for h in range(nh):
        core = h % 2
        for x in range(nx):
            for z in range(nz):
                near, far = place((x + nx - core) % nx, (z + nz - core) % nz, nz)
                device = (x * nz + z) * nh + h
                squares.setdefault((h, far), {})[near] = device
                likes.setdefault((h, near), {})[far] = device
    ordered = lambda groups: [[g[i] for i in range(len(g))] for g in groups.values()]
    return ordered(squares), ordered(likes)


def exchange(v, groups):
    return lax.all_to_all(
        v, MESH_AXES, split_axis=0, concat_axis=0, axis_index_groups=groups, tiled=True
    )


def in_vmem(v):
    return pltpu.with_memory_space_constraint(v, pltpu.VMEM)


def shape(dims, dtype):
    return jax.ShapeDtypeStruct(dims, dtype)


def on_device(acts, queries, keys, values, out_grad):
    toks, width = queries.shape
    nblocks = lax.axis_size(CTX)
    scale = float(toks * nblocks) ** (-0.5)
    pieces = 2 * width // 8
    heads = width // DH
    of_head = pl.BlockSpec((toks, DH), lambda h: (0, h))
    st = pl.pallas_call(
        states_kernel,
        grid=(heads,),
        in_specs=[of_head] * 4,
        out_specs=pl.BlockSpec((2, DH // 8, 8, DH), lambda h: (0, h, 0, 0)),
        out_shape=shape((2, heads * DH // 8, 8, DH), F32),
        name="states",
    )(queries, keys, values, out_grad).reshape(pieces, 8, DH)
    rows = acts.shape[1]
    nx, nz, nh = (lax.axis_size(a) for a in MESH_AXES)
    step = rows // nx
    own = rows // nblocks
    core = (lax.axis_index("head") % 2).astype(jnp.int32).reshape(1)
    whole = lambda *dims: pl.BlockSpec(dims, lambda i: (0,) * len(dims))
    cut = (4, nblocks // 4, own)
    half = (cut[0] // 2,) + cut[1:] + (toks,)
    kept, turned = pl.pallas_call(
        turn_kernel,
        grid=(nx,),
        in_specs=[
            pl.BlockSpec(memory_space=pltpu.SMEM),
            pl.BlockSpec((toks, step), lambda i: (0, i)),
        ],
        out_specs=(IN_VMEM, whole(*half)),
        out_shape=(pltpu.VMEM(half, BF16), shape(half, BF16)),
        name="turn",
    )(core, acts)
    received = lax.all_to_all(st, CTX, split_axis=0, concat_axis=0, tiled=True)
    back = (lax.axis_index(CTX) >= nblocks // 2).astype(jnp.int32).reshape(1)
    answers = pl.pallas_call(
        scan_kernel,
        in_specs=[
            pl.BlockSpec(memory_space=pltpu.SMEM),
            IN_VMEM,
            pl.BlockSpec(memory_space=pl.ANY),
        ],
        out_shape=shape((nblocks, 8, DH), BF16),
        name="scan",
    )(back, in_vmem(received), turned)
    low = lax.all_to_all(answers, CTX, split_axis=0, concat_axis=0, tiled=True)
    low = in_vmem(low)
    part = shape((toks, width), F32)
    lq, lk, lv, kn = pl.pallas_call(
        functools.partial(local_kernel, scale),
        out_shape=(part, part, pltpu.VMEM((toks, width), F32), pltpu.VMEM((toks, width), BF16)),
        name="local",
    )(queries, keys, values, out_grad)
    anywhere = pl.BlockSpec(memory_space=pl.ANY)
    dv_out, w = pl.pallas_call(
        functools.partial(weights_kernel, scale),
        in_specs=[IN_VMEM, anywhere, IN_VMEM, IN_VMEM, IN_VMEM],
        out_specs=(anywhere, anywhere),
        out_shape=(shape((toks, width), BF16), shape((rows, width), BF16)),
        scratch_shapes=[
            pltpu.VMEM((rows // 2, toks), BF16),
            pltpu.VMEM((toks, width), BF16),
            pltpu.VMEM((rows, width), BF16),
            pltpu.SemaphoreType.DMA((nx // 2,)),
            pltpu.SemaphoreType.DMA((nx + 1,)),
        ],
        name="weights",
    )(in_vmem(kept.reshape(rows // 2, toks)), turned.reshape(rows // 2, toks), in_vmem(kn), in_vmem(lv), low)
    w = w.reshape(*cut, width)
    first, second = core_groups(nx, nz, nh)
    got = exchange(w, first)
    got = jnp.sum(got.astype(F32), axis=0).astype(BF16)
    got = exchange(got, second)
    wv = jnp.sum(got.astype(F32), axis=0)
    dq_out, dk_out = pl.pallas_call(
        functools.partial(back_kernel, scale),
        in_specs=[IN_VMEM] * 7,
        out_shape=(shape((toks, width), BF16),) * 2,
        name="back",
    )(queries, keys, values, out_grad, lq, lk, low)
    return dq_out, dk_out, dv_out, wv


def solution(mesh):
    finer = Mesh(mesh.devices.reshape(*ROW_CUTS, mesh.shape["head"]), ("ctx_0", "ctx_1", "head"))
    return jax.shard_map(
        on_device,
        mesh=finer,
        in_specs=(P(CTX, None), P(CTX, "head"), P(CTX, "head"), P(CTX, "head"), P(CTX, "head")),
        out_specs=(P(CTX, "head"), P(CTX, "head"), P(CTX, "head"), P(CTX, "head")),
        check_vma=False,
    )
```

```python
import functools

import jax
import jax.numpy as jnp
from jax import lax
from jax.experimental import pallas as pl
from jax.experimental.pallas import tpu as pltpu
from jax.sharding import Mesh
from jax.sharding import PartitionSpec as P

DH = 128
CTX = ("ctx_0", "ctx_1")
MESH_AXES = CTX + ("head",)
ROW_CUTS = (8, 8)
IN_VMEM = pl.BlockSpec(memory_space=pltpu.VMEM)
F32 = jnp.float32
BF16 = jnp.bfloat16


def dot(a, b, ca, cb):
    return lax.dot_general(a, b, (((ca,), (cb,)), ((), ())), preferred_element_type=F32)


def unit_of(block):
    full = block.astype(F32)
    factor = lax.rsqrt(jnp.sum(full * full, axis=-1, keepdims=True) + 1e-06)
    return full * factor, factor


def head(ref, h):
    return ref[:, h * DH : (h + 1) * DH]


def states_kernel(q_ref, k_ref, v_ref, o_ref, st_ref):
    kn = unit_of(k_ref[...])[0].astype(BF16)
    qn = unit_of(q_ref[...])[0].astype(BF16)
    st_ref[0] = dot(kn, v_ref[...], 0, 0).reshape(st_ref.shape[1:]).astype(BF16)
    st_ref[1] = dot(qn, o_ref[...], 0, 0).reshape(st_ref.shape[1:]).astype(BF16)


def scan_kernel(back_ref, r_ref, after_ref, out_ref):
    del after_ref
    n = r_ref.shape[0]
    back = back_ref[0]

    def step(i, acc):
        b = jnp.where(back == 1, n - 1 - i, i)
        out_ref[b] = acc.astype(out_ref.dtype)
        return acc + r_ref[b].astype(F32)

    lax.fori_loop(0, n, step, jnp.zeros(r_ref.shape[1:], F32), unroll=8)


def local_kernel(scale, q_ref, k_ref, v_ref, o_ref, dq_ref, dk_ref, dv_ref, kn_ref):
    toks, width = q_ref.shape
    mask = lax.broadcasted_iota(jnp.int32, (toks, toks), 0) >= lax.broadcasted_iota(
        jnp.int32, (toks, toks), 1
    )
    for h in range(width // DH):
        at = slice(h * DH, (h + 1) * DH)
        kn = unit_of(head(k_ref, h))[0].astype(BF16)
        kn_ref[:, at] = kn
        qn = unit_of(head(q_ref, h))[0].astype(BF16)
        v, o = head(v_ref, h), head(o_ref, h)
        attn = jnp.where(mask, dot(qn, kn, 1, 1) * scale, 0.0).astype(BF16)
        dv_ref[:, at] = dot(attn, o, 0, 0)
        scores = jnp.where(mask, dot(o, v, 1, 1) * scale, 0.0).astype(BF16)
        dq_ref[:, at] = dot(scores, kn, 1, 0)
        dk_ref[:, at] = dot(scores, qn, 0, 0)


def state(st_ref, kind, h):
    heads = st_ref.shape[0] // 2 // (DH // 8)
    rows = DH // 8
    at = (kind * heads + h) * rows
    return st_ref[at : at + rows].astype(F32).reshape(DH, DH).astype(BF16)


def turn_kernel(core_ref, acts_ref, kept_ref, out_ref):
    x = pl.program_id(0)
    nx = pl.num_programs(0)
    nz, own = ROW_CUTS[1], out_ref.shape[2]
    half = out_ref.shape[0]
    turned = acts_ref[...].T.reshape(nz, own, acts_ref.shape[0])
    for core in range(2):
        for z in range(nz):
            near, far = place(lax.rem(x + nx - core, nx), (z + nz - core) % nz, nz)

            @pl.when((core_ref[0] == core) & (near < half))
            def _():
                kept_ref[near, far] = turned[z]

            @pl.when((core_ref[0] == core) & (near >= half))
            def _():
                out_ref[near - half, far] = turned[z]


def weights_kernel(
    scale, kept_ref, turned_ref, kn_ref, loc_ref, st_ref, dv_ref, w_ref, rows_ref, low_ref, sums_ref, come, go
):
    n = come.shape[0]
    step = rows_ref.shape[0] // n
    at_step = lambda i: pl.ds(i * step, step)
    coming = [
        pltpu.make_async_copy(turned_ref.at[at_step(i)], rows_ref.at[at_step(i)], come.at[i])
        for i in range(n)
    ]
    going = [
        pltpu.make_async_copy(sums_ref.at[at_step(i)], w_ref.at[at_step(i)], go.at[i])
        for i in range(2 * n)
    ]
    for copy in coming:
        copy.start()
    for h in range(kn_ref.shape[1] // DH):
        at = slice(h * DH, (h + 1) * DH)
        dvv = loc_ref[:, at] + scale * dot(head(kn_ref, h), state(st_ref, 1, h), 1, 0)
        low_ref[:, at] = dvv.astype(BF16)
    keep = pltpu.make_async_copy(low_ref, dv_ref, go.at[2 * n])
    keep.start()
    for i in range(2 * n):
        if i < n:
            rows = kept_ref[at_step(i)]
        else:
            coming[i - n].wait()
            rows = rows_ref[at_step(i - n)]
        sums_ref[at_step(i)] = dot(rows, low_ref[...], 1, 0).astype(BF16)
        going[i].start()
    for copy in going:
        copy.wait()
    keep.wait()


def back_kernel(scale, q_ref, k_ref, v_ref, o_ref, lq_ref, lk_ref, st_ref, dq_ref, dk_ref):
    for h in range(q_ref.shape[1] // DH):
        at = slice(h * DH, (h + 1) * DH)
        for src, other, loc, kind, out in (
            (q_ref, o_ref, lq_ref, 0, dq_ref),
            (k_ref, v_ref, lk_ref, 1, dk_ref),
        ):
            unit, factor = unit_of(head(src, h))
            grad = loc[:, at] + scale * dot(head(other, h), state(st_ref, kind, h), 1, 1)
            inner = jnp.sum(unit * grad, axis=-1, keepdims=True)
            out[:, at] = (factor * (grad - unit * inner)).astype(BF16)


def place(x, z, nz):
    flip = nz // 2
    return (
        (x + x // flip) % 2 * 2 + (z + z // flip) % 2,
        x // 2 * (nz // 2) + z // 2,
    )


def core_groups(nx, nz, nh):
    squares, likes = {}, {}
    for h in range(nh):
        core = h % 2
        for x in range(nx):
            for z in range(nz):
                near, far = place((x + nx - core) % nx, (z + nz - core) % nz, nz)
                device = (x * nz + z) * nh + h
                squares.setdefault((h, far), {})[near] = device
                likes.setdefault((h, near), {})[far] = device
    ordered = lambda groups: [[g[i] for i in range(len(g))] for g in groups.values()]
    return ordered(squares), ordered(likes)


def exchange(v, groups):
    return lax.all_to_all(
        v, MESH_AXES, split_axis=0, concat_axis=0, axis_index_groups=groups, tiled=True
    )


def in_vmem(v):
    return pltpu.with_memory_space_constraint(v, pltpu.VMEM)


def shape(dims, dtype):
    return jax.ShapeDtypeStruct(dims, dtype)


def on_device(acts, queries, keys, values, out_grad):
    toks, width = queries.shape
    nblocks = lax.axis_size(CTX)
    scale = float(toks * nblocks) ** (-0.5)
    pieces = 2 * width // 8
    heads = width // DH
    of_head = pl.BlockSpec((toks, DH), lambda h: (0, h))
    st = pl.pallas_call(
        states_kernel,
        grid=(heads,),
        in_specs=[of_head] * 4,
        out_specs=pl.BlockSpec((2, DH // 8, 8, DH), lambda h: (0, h, 0, 0)),
        out_shape=shape((2, heads * DH // 8, 8, DH), BF16),
        name="states",
    )(queries, keys, values, out_grad).reshape(pieces, 8, DH)
    rows = acts.shape[1]
    nx, nz, nh = (lax.axis_size(a) for a in MESH_AXES)
    step = rows // nx
    own = rows // nblocks
    core = (lax.axis_index("head") % 2).astype(jnp.int32).reshape(1)
    whole = lambda *dims: pl.BlockSpec(dims, lambda i: (0,) * len(dims))
    cut = (4, nblocks // 4, own)
    half = (cut[0] // 2,) + cut[1:] + (toks,)
    kept, turned = pl.pallas_call(
        turn_kernel,
        grid=(nx,),
        in_specs=[
            pl.BlockSpec(memory_space=pltpu.SMEM),
            pl.BlockSpec((toks, step), lambda i: (0, i)),
        ],
        out_specs=(IN_VMEM, whole(*half)),
        out_shape=(pltpu.VMEM(half, BF16), shape(half, BF16)),
        name="turn",
    )(core, acts)
    received = lax.all_to_all(st, CTX, split_axis=0, concat_axis=0, tiled=True)
    back = (lax.axis_index(CTX) >= nblocks // 2).astype(jnp.int32).reshape(1)
    answers = pl.pallas_call(
        scan_kernel,
        in_specs=[
            pl.BlockSpec(memory_space=pltpu.SMEM),
            IN_VMEM,
            pl.BlockSpec(memory_space=pl.ANY),
        ],
        out_shape=shape((nblocks, 8, DH), BF16),
        name="scan",
    )(back, in_vmem(received), turned)
    low = lax.all_to_all(answers, CTX, split_axis=0, concat_axis=0, tiled=True)
    low = in_vmem(low)
    part = shape((toks, width), F32)
    lq, lk, lv, kn = pl.pallas_call(
        functools.partial(local_kernel, scale),
        out_shape=(part, part, pltpu.VMEM((toks, width), F32), pltpu.VMEM((toks, width), BF16)),
        name="local",
    )(queries, keys, values, out_grad)
    anywhere = pl.BlockSpec(memory_space=pl.ANY)
    dv_out, w = pl.pallas_call(
        functools.partial(weights_kernel, scale),
        in_specs=[IN_VMEM, anywhere, IN_VMEM, IN_VMEM, IN_VMEM],
        out_specs=(anywhere, anywhere),
        out_shape=(shape((toks, width), BF16), shape((rows, width), BF16)),
        scratch_shapes=[
            pltpu.VMEM((rows // 2, toks), BF16),
            pltpu.VMEM((toks, width), BF16),
            pltpu.VMEM((rows, width), BF16),
            pltpu.SemaphoreType.DMA((nx // 2,)),
            pltpu.SemaphoreType.DMA((nx + 1,)),
        ],
        name="weights",
    )(in_vmem(kept.reshape(rows // 2, toks)), turned.reshape(rows // 2, toks), in_vmem(kn), in_vmem(lv), low)
    w = w.reshape(*cut, width)
    first, second = core_groups(nx, nz, nh)
    got = exchange(w, first)
    got = jnp.sum(got.astype(F32), axis=0).astype(BF16)
    got = exchange(got, second)
    wv = jnp.sum(got.astype(F32), axis=0)
    dq_out, dk_out = pl.pallas_call(
        functools.partial(back_kernel, scale),
        in_specs=[IN_VMEM] * 7,
        out_shape=(shape((toks, width), BF16),) * 2,
        name="back",
    )(queries, keys, values, out_grad, lq, lk, low)
    return dq_out, dk_out, dv_out, wv


def solution(mesh):
    finer = Mesh(mesh.devices.reshape(*ROW_CUTS, mesh.shape["head"]), ("ctx_0", "ctx_1", "head"))
    return jax.shard_map(
        on_device,
        mesh=finer,
        in_specs=(P(CTX, None), P(CTX, "head"), P(CTX, "head"), P(CTX, "head"), P(CTX, "head")),
        out_specs=(P(CTX, "head"), P(CTX, "head"), P(CTX, "head"), P(CTX, "head")),
        check_vma=False,
    )
```
